32 devices in a mesh: row: 8 (over y, x, core), col: 4 (over z).
Axes of the slice: x: 2, y: 2, z: 4, core: 2. Of those that a mesh axis runs over, the one named last changes fastest.
Arguments:
- factor: bfloat16 [64, 16, 128, 128], P('row', 'col'), may hold values from -0.1796875 to 0.1796875
- inverse_pivot: float32 [64, 128], P('row'), may hold values from 0.5 to 2
- lower_rhs: float32 [16, 64, 128], P(None, 'col'), may hold values from -6 to 6
- upper_rhs: float32 [16, 64, 128], P(None, 'col'), may hold values from -6 to 6
- snode_of_block: int32 [64], replicated, may hold values from 0 to 15, as said below
- level_of_snode: int32 [16], replicated, may hold values from 0 to 5, as said below
- slot_columns: int32 [64, 16], P('row', 'col'), may hold values from 0 to 64, as said below
Outputs:
- lower_solution: float32 [16, 64, 128], P(None, 'row')
- upper_solution: float32 [16, 64, 128], P(None, 'row')
The draws below stay inside these ranges and needn't reach their ends.
Inputs may be any that keep to these rules, and one draw needn't show every extreme that they name: `snode_of_block`: never falling along the blocks, starting at 0 and rising by at most one; every supernode covers an even number of blocks. `level_of_snode`: never falling along the supernodes, starting at 0 and rising by at most one; every level holds one or more supernodes, the top level exactly one, the last. `slot_columns`: the slots of process column c name distinct blocks J with J % 4 == c, or 64; every block row names its own block; a named J lies in the row's supernode or in one that is an ancestor or descendant of it in the elimination tree, in which every supernode below the top level has its parent one level up; some block row fills all 4 slots of some process column.
All inputs are finite; a program needn't handle non-finite values.
Results may differ from the reference program's by a relative error of at most 0.0059.
Values may be sent and summed in bfloat16 or wider, within the bound.
No kernel may reach another device: no remote copies, remote signals or barrier semaphores. Data moves between devices by JAX's collectives and lax.ppermute only.
A program may use at most 128 MiB of HBM per device.

```python
import math
import jax
import jax.numpy as jnp
from jax import lax

B = 128
BR = 8
KC = 4
NRHS = 16
NB = 64
BC = 16
SNODES = 16
LEVELS = 6
N_COL = 4


def structure(key):
    base_key = jax.random.fold_in(key, 41)
    cut_key, level_key, parent_key, coin_key, score_key = jax.random.split(base_key, 5)
    pair_count = NB // 2
    cut_rank = jax.random.permutation(cut_key, pair_count - 1)
    cut_flags = (cut_rank < SNODES - 1).astype(jnp.int32)
    pair_snode = jnp.concatenate([jnp.zeros((1,), jnp.int32), jnp.cumsum(cut_flags).astype(jnp.int32)])
    block_snode = jnp.repeat(pair_snode, 2).astype(jnp.int32)
    level_rank = jax.random.permutation(level_key, SNODES - 2)
    level_flags = (level_rank < LEVELS - 2).astype(jnp.int32)
    lower_levels = jnp.concatenate([jnp.zeros((1,), jnp.int32), jnp.cumsum(level_flags).astype(jnp.int32)])
    snode_level = jnp.concatenate([lower_levels, jnp.full((1,), LEVELS - 1, jnp.int32)])
    level_ids = jnp.arange(LEVELS, dtype=jnp.int32)
    member = (snode_level[:, None] == level_ids[None, :]).astype(jnp.int32)
    level_sizes = jnp.sum(member, axis=0).astype(jnp.int32)
    level_starts = (jnp.cumsum(level_sizes) - level_sizes).astype(jnp.int32)
    next_level = jnp.minimum(snode_level + 1, LEVELS - 1)
    next_onehot = (next_level[:, None] == level_ids[None, :]).astype(jnp.int32)
    next_size = jnp.sum(next_onehot * level_sizes[None, :], axis=1).astype(jnp.int32)
    next_start = jnp.sum(next_onehot * level_starts[None, :], axis=1).astype(jnp.int32)
    random_picks = jax.random.randint(parent_key, (SNODES,), 0, 1 << 20).astype(jnp.int32)
    parent = next_start + random_picks % next_size
    has_parent = snode_level < LEVELS - 1
    snode_ids = jnp.arange(SNODES, dtype=jnp.int32)
    step_matrix = ((snode_ids[None, :] == parent[:, None]) & has_parent[:, None]).astype(jnp.int32)
    ancestors = step_matrix
    reached = step_matrix
    for distance in range(LEVELS - 2):
        reached = (jnp.dot(reached, step_matrix) > 0).astype(jnp.int32)
        ancestors = jnp.maximum(ancestors, reached)
    related = jnp.maximum(ancestors, ancestors.T)
    block_related = related[block_snode][:, block_snode]
    coin_flips = jax.random.randint(coin_key, (NB, NB), 0, 2).astype(jnp.int32)
    block_ids = jnp.arange(NB, dtype=jnp.int32)
    coin_flips = jnp.where(block_ids[:, None] < block_ids[None, :], coin_flips, coin_flips.T)
    is_root = block_snode == SNODES - 1
    coin_flips = jnp.where(is_root[:, None] | is_root[None, :], 1, coin_flips)
    same_snode = block_snode[:, None] == block_snode[None, :]
    candidate = jnp.where(same_snode, 1, block_related * coin_flips).astype(jnp.int32)
    diag = (block_ids[:, None] == block_ids[None, :]).astype(jnp.int32)
    big = NB * NB
    tie_break = jax.random.permutation(score_key, big).astype(jnp.int32).reshape(NB, NB)
    score = candidate * (4 * big) + diag * (2 * big) + same_snode.astype(jnp.int32) * big + tie_break
    by_class = jnp.transpose(score.reshape(NB, BC, N_COL), (0, 2, 1))
    cand_class = jnp.transpose(candidate.reshape(NB, BC, N_COL), (0, 2, 1))
    chosen_score, chosen = lax.top_k(by_class, KC)
    chosen = chosen.astype(jnp.int32)
    chosen_cand = jnp.take_along_axis(cand_class, chosen, axis=2)
    class_ids = jnp.arange(N_COL, dtype=jnp.int32)
    natural = chosen * N_COL + class_ids[None, :, None]
    slots = jnp.where(chosen_cand > 0, natural, NB).astype(jnp.int32).reshape(NB, N_COL * KC)
    row_order = (block_ids % BR * (NB // BR) + block_ids // BR).astype(jnp.int32)
    return (block_snode, snode_level, jnp.take(slots, row_order, axis=0).astype(jnp.int32))


def draw_snode_of_block(key, part):
    return structure(key)[0]


def draw_level_of_snode(key, part):
    return structure(key)[1]


def draw_slot_columns(key, part):
    return structure(key)[2]


def steps_of(own_key, dims, shards, smallest, largest):
    gain, own = 1.0, jax.random.fold_in(own_key, 6)
    for dim, shards_of in shards:
        heights = jnp.exp(jax.random.uniform(jax.random.fold_in(own, dim), (shards_of,), jnp.float32, smallest / len(shards), largest / len(shards)))
        gain = gain * jnp.repeat(heights, dims[dim] // shards_of).reshape([-1 if axis == dim else 1 for axis in range(len(dims))])
    return gain


def scatter_about(rng, dims, scale, most, cuts=(), kind=jnp.bfloat16):
    result = jax.random.normal(rng, dims, jnp.float32) * scale
    if len(cuts) > 0:
        result = steps_of(rng, dims, cuts, -0.22, 0.18) * result
    return jnp.clip(result, min=-most, max=most).astype(kind)


def setup_inputs(seed: int = 0) -> dict:
    keys = jax.random.split(jax.random.key(seed), 8)
    return {
        "factor": scatter_about(keys[0], (NB, N_COL * KC, B, B), 0.03, 0.1796875, ((0, 8), (1, 4))),
        "inverse_pivot": jnp.clip(jnp.exp(math.log(2.0) - 1.3862944 * jax.random.uniform(keys[1], (NB, B), jnp.float32) ** steps_of(keys[1], (NB, B), ((0, 8),), -0.2, 0.2)), 0.5, 2.0),
        "lower_rhs": scatter_about(keys[2], (NRHS, NB, B), 1.0, 6.0, ((1, 4),), jnp.float32),
        "upper_rhs": scatter_about(keys[3], (NRHS, NB, B), 1.0, 6.0, ((1, 4),), jnp.float32),
        "snode_of_block": draw_snode_of_block(jax.random.fold_in(keys[7], 71), 0),
        "level_of_snode": draw_level_of_snode(jax.random.fold_in(keys[7], 71), 0),
        "slot_columns": draw_slot_columns(jax.random.fold_in(keys[7], 71), 0),
    }


def block_levels(snode_of_block, level_of_snode):
    onehot = snode_of_block[:, None] == jnp.arange(SNODES, dtype=jnp.int32)[None, :]
    return jnp.sum(jnp.where(onehot, level_of_snode[None, :], 0), axis=1).astype(jnp.int32)


def column_position(block):
    return ((block % N_COL) * BC + block // N_COL).astype(jnp.int32)


def reference(factor, inverse_pivot, lower_rhs, upper_rhs, snode_of_block, level_of_snode, slot_columns):
    row_count = NB // BR
    col_count = NB // BC
    blocks = jnp.arange(NB, dtype=jnp.int32)
    levels = block_levels(snode_of_block, level_of_snode)
    col_blocks = ((blocks % BC) * col_count + blocks // BC).astype(jnp.int32)
    row_blocks = ((blocks % BR) * row_count + blocks // BR).astype(jnp.int32)
    col_levels = levels[col_blocks]
    strict_low = jnp.tril(jnp.ones((B, B), jnp.float32), -1)
    strict_up = jnp.triu(jnp.ones((B, B), jnp.float32), 1)
    high = lax.Precision.HIGHEST

    def products(lower_in, upper_in):
        lower_f = lower_in.astype(jnp.float32)
        upper_f = upper_in.astype(jnp.float32)

        def row_terms(row_block):
            position = ((row_block % row_count) * BR + row_block // row_count).astype(jnp.int32)
            row_panel = lax.dynamic_index_in_dim(factor, position, 0, keepdims=False).astype(jnp.float32)
            slot_ids = lax.dynamic_index_in_dim(slot_columns, position, 0, keepdims=False)
            valid = slot_ids < NB
            safe = jnp.minimum(slot_ids, NB - 1).astype(jnp.int32)
            own_snode = lax.dynamic_index_in_dim(snode_of_block, row_block, 0, keepdims=False)
            own_level = lax.dynamic_index_in_dim(levels, row_block, 0, keepdims=False)
            same = jnp.take(snode_of_block, safe) == own_snode
            slot_level = jnp.take(levels, safe)
            lower_s = valid & jnp.where(same, safe < row_block, own_level > slot_level)
            upper_s = valid & jnp.where(same, safe > row_block, own_level < slot_level)
            diag_s = valid & (safe == row_block)
            lower_w = jnp.where(diag_s[:, None, None], strict_low[None], lower_s.astype(jnp.float32)[:, None, None])
            upper_w = jnp.where(diag_s[:, None, None], strict_up[None], upper_s.astype(jnp.float32)[:, None, None])
            places = column_position(safe)
            lower_pick = jnp.take(lower_f, places, axis=1)
            upper_pick = jnp.take(upper_f, places, axis=1)
            lower_terms = jnp.einsum("ksj,sij->ki", lower_pick, row_panel * lower_w, precision=high)
            upper_terms = jnp.einsum("ksj,sij->ki", upper_pick, row_panel * upper_w, precision=high)
            own_place = column_position(row_block)
            lower_own = lax.dynamic_index_in_dim(lower_f, own_place, 1, keepdims=False)
            upper_own = lax.dynamic_index_in_dim(upper_f, own_place, 1, keepdims=False)
            pivot_row = lax.dynamic_index_in_dim(inverse_pivot, position, 0, keepdims=False)
            return lower_terms + lower_own, upper_terms + pivot_row[None, :] * upper_own

        lower_all, upper_all = lax.map(row_terms, blocks)
        return jnp.transpose(lower_all, (1, 0, 2)), jnp.transpose(upper_all, (1, 0, 2))

    lower_res = lower_rhs
    upper_res = upper_rhs
    lower_sol = jnp.zeros((NRHS, NB, B), jnp.float32)
    upper_sol = jnp.zeros((NRHS, NB, B), jnp.float32)
    for level_step in range(LEVELS):
        lower_level = level_step
        upper_level = LEVELS - 1 - level_step
        lower_in = jnp.where((col_levels == lower_level)[None, :, None], lower_res, 0.0).astype(jnp.bfloat16)
        upper_in = jnp.where((col_levels == upper_level)[None, :, None], upper_res, 0.0).astype(jnp.bfloat16)
        lower_sum, upper_sum = products(lower_in, upper_in)
        lower_new = jnp.where((levels == lower_level)[None, :, None], lower_sum, 0.0)
        upper_new = jnp.where((levels == upper_level)[None, :, None], upper_sum, 0.0)
        lower_sol = lower_sol + lower_new
        upper_sol = upper_sol + upper_new
        if level_step + 1 < LEVELS:
            lower_upd, upper_upd = products(lower_new.astype(jnp.bfloat16)[:, col_blocks], upper_new.astype(jnp.bfloat16)[:, col_blocks])
            lower_back = jnp.where((levels > lower_level)[None, :, None], lower_upd, 0.0).astype(jnp.bfloat16)
            upper_back = jnp.where((levels < upper_level)[None, :, None], upper_upd, 0.0).astype(jnp.bfloat16)
            lower_res = lower_res - lower_back[:, col_blocks].astype(jnp.float32)
            upper_res = upper_res - upper_back[:, col_blocks].astype(jnp.float32)
    return lower_sol[:, row_blocks], upper_sol[:, row_blocks]
```

```python
import functools

import jax
import jax.numpy as jnp
from jax import lax
from jax.experimental import pallas as pl
from jax.experimental.pallas import tpu as pltpu
from jax.sharding import PartitionSpec as P


def xor_permute(value, axis, distance):
    size = lax.axis_size(axis)
    return lax.ppermute(value, axis, [(i, i ^ distance) for i in range(size)])


def bits_of(size):
    return [1 << b for b in range(size.bit_length() - 1)]


def gather_rows(factor):
    size = lax.axis_size("row")
    half = factor.shape[0] // 2
    pieces = {0: (factor[:half], factor[half:])}
    for k in range(2, size, 2):
        high = 1 << (k.bit_length() - 1)
        low = k & -k
        pieces[k] = (
            xor_permute(pieces[k ^ high][0], "row", high),
            xor_permute(pieces[k ^ low][1], "row", low),
        )
    for k in range(0, size, 2):
        pieces[k ^ 1] = tuple(xor_permute(part, "row", 1) for part in pieces[k])
    return [part for k in range(size) for part in pieces[k]]


def prepare_diagonal(scalars, dims, parts):
    rows, cols, groups, per_row, slots, block = dims
    half = per_row // 2

    def body(*refs):
        sc, slot_of = refs[0], refs[1]
        part_refs = refs[2:2 + 2 * rows]
        out = refs[2 + 2 * rows]
        here = sc[0]
        row_high = sc[1]
        op = sc[2]
        row_i = lax.broadcasted_iota(jnp.int32, (block, block), 0)
        col_i = lax.broadcasted_iota(jnp.int32, (block, block), 1)
        ahead = jnp.where(op == 0, row_i - col_i, col_i - row_i) > 0
        for k in range(rows):
            @pl.when(here == k % cols)
            def _(k=k):
                m = row_high ^ (k // cols)
                for i in range(per_row):
                    source = part_refs[2 * k + i // half]
                    s = slot_of[m * per_row + i]
                    value = source[i % half, s].astype(jnp.float32)
                    out[m, i] = jnp.where(ahead, value, 0.0).astype(out.dtype)

    vmem = pl.BlockSpec(memory_space=pltpu.VMEM)
    smem = pl.BlockSpec(memory_space=pltpu.SMEM)
    return pl.pallas_call(
        body,
        out_shape=jax.ShapeDtypeStruct((groups, per_row, block, block), parts[0].dtype),
        in_specs=[smem, smem] + [vmem] * len(parts),
        out_specs=vmem,
        name="prepare_diagonal",
    )(scalars[0], scalars[1], *parts)


def step_kernel(kind, step, dims, scalars, table, parts, diag, level, pivot, state, received):
    rows, cols, groups, per_row, slots, block, kept = dims
    half = per_row // 2
    lanes = groups * kept
    locals_here = per_row * groups
    flat = (per_row * lanes, block)
    tile = (per_row, lanes, block)

    def body(*refs):
        refs = list(refs)
        sc = refs.pop(0)
        idx = refs.pop(0)
        part_refs = [refs.pop(0) for _ in parts]
        diag_ref = refs.pop(0)
        level_ref = refs.pop(0)
        pivot_ref = refs.pop(0)
        res_ref = refs.pop(0)
        sol_ref = refs.pop(0)
        got = [refs.pop(0) for _ in received]
        if kind == "last":
            out_sol = refs.pop(0)
        else:
            sends = [refs.pop(0) for _ in range(cols)]
            out_state = refs.pop(0)
            xs, acc = refs
        lv = level_ref[...]
        res = res_ref[...]
        if got:
            total = got[0][...]
            for ref in got[1:]:
                total = total + ref[...].astype(jnp.float32)
        if kind in ("solved", "last"):
            rounded = res.astype(jnp.bfloat16).astype(jnp.float32)
            y = jnp.where(lv == step, total + pivot_ref[...] * rounded, 0.0)
            sol = sol_ref[...] + y
            if kind == "last":
                out_sol[...] = sol
                return
            out_state[...] = sol
            source = y
        elif kind == "updated":
            back = total.astype(jnp.bfloat16).astype(jnp.float32)
            res = jnp.where(lv > step, res - back, res)
            out_state[...] = res
            source = jnp.where(lv == step + 1, res, 0.0)
        else:
            out_state[...] = res
            source = jnp.where(lv == 0, res, 0.0)
        source = source.reshape(tile)
        lane_group = lax.broadcasted_iota(jnp.int32, (1, lanes, block), 1) // kept
        for shift in range(groups):
            moved = source
            if shift:
                moved = jnp.concatenate([source[:, lanes - shift * kept:], source[:, :lanes - shift * kept]], axis=1)
            for m in range(groups):
                mine = (m + groups - shift) % groups
                put = jnp.where(lane_group == m, moved, 0.0)
                for i in range(per_row):
                    xs[m, i * groups + mine] = put[i]
        for m in range(groups):
            xs[m, locals_here] = jnp.zeros((lanes, block), jnp.float32)
        acc[...] = jnp.zeros(acc.shape, jnp.float32)
        here = sc[0]
        row_high = sc[1]
        which = 3 + 4 * (step + (1 if kind == "updated" else 0)) + (2 if kind == "solved" else 0)
        low = sc[which]
        high = sc[which + 1]

        def contract(x, w):
            return lax.dot_general(
                x.astype(jnp.bfloat16), w, (((1,), (1,)), ((), ())), preferred_element_type=jnp.float32
            )

        def group(i, part):
            for kk in range(cols):
                value = None
                for mm in range(groups):
                    k = kk + cols * mm
                    m = row_high ^ mm
                    for s in range(slots):
                        j = idx[(k * per_row + i) * slots + s]
                        term = contract(xs[m, j], part_refs[2 * k + part][i - part * half, s])
                        value = term if value is None else value + term
                acc[here ^ kk, i] = value
            own = acc[0, i]
            for m in range(groups):
                own = own + contract(xs[m, i * groups + m], diag_ref[m, i])
            acc[0, i] = own

        for part in range(2):
            begin = jnp.maximum(low, part * half)
            end = jnp.minimum(high, (part + 1) * half)

            def loop(i, carry, part=part):
                group(i, part)
                return carry

            lax.fori_loop(begin, end, loop, 0)
        sends[0][...] = acc[0].reshape(flat)
        for d in range(1, cols):
            sends[d][...] = acc[d].reshape(flat).astype(sends[d].dtype)

    vmem = pl.BlockSpec(memory_space=pltpu.VMEM)
    smem = pl.BlockSpec(memory_space=pltpu.SMEM)
    args = [scalars, table, *parts, diag, level, pivot, *state, *received]
    if kind == "last":
        out_shape = jax.ShapeDtypeStruct(flat, jnp.float32)
        out_specs = vmem
        scratch = []
    else:
        out_shape = (
            [jax.ShapeDtypeStruct(flat, jnp.float32)]
            + [jax.ShapeDtypeStruct(flat, jnp.bfloat16)] * (cols - 1)
            + [jax.ShapeDtypeStruct(flat, jnp.float32)]
        )
        out_specs = [vmem] * (cols + 1)
        scratch = [
            pltpu.VMEM((groups, locals_here + 1, lanes, block), jnp.float32),
            pltpu.VMEM((cols, per_row, lanes, block), jnp.float32),
        ]
    return pl.pallas_call(
        body,
        out_shape=out_shape,
        in_specs=[smem, smem] + [vmem] * (len(args) - 2),
        out_specs=out_specs,
        scratch_shapes=scratch,
        name="step_" + kind,
    )(*args)


def shards(
    factor, inverse_pivot, lower_rhs, upper_rhs, snode_of_block, level_of_snode, slot_columns
):
    rows = lax.axis_size("row")
    cols = lax.axis_size("col")
    r = lax.axis_index("row")
    c = lax.axis_index("col")
    per_row, slots, block = factor.shape[:3]
    total = snode_of_block.shape[0]
    snodes = level_of_snode.shape[0]
    rhs_count = lower_rhs.shape[0]
    steps = min(6, snodes // 2)
    groups = rows // cols
    kept = 2 * rhs_count // rows
    locals_here = per_row * groups
    lanes = groups * kept
    op = r % 2
    dims = (rows, cols, groups, per_row, slots, block)

    small = jnp.concatenate(
        [inverse_pivot, jnp.pad(slot_columns.astype(jnp.float32), ((0, 0), (0, block - slots)))], axis=1
    )[None]
    for bit in bits_of(rows):
        small = jnp.concatenate([small, xor_permute(small, "row", bit)], axis=0)
    parts = gather_rows(factor)

    blocks = jnp.arange(total, dtype=jnp.int32)
    onehot = snode_of_block[:, None] == jnp.arange(snodes, dtype=jnp.int32)[None, :]
    levels = jnp.sum(jnp.where(onehot, level_of_snode[None, :], 0), axis=1)
    levels = jnp.where(op == 0, levels, steps - 1 - levels)

    def look_up(values, index):
        return jnp.sum(jnp.where(index[..., None] == blocks, values, 0), axis=-1)

    slot_ids = small[:, :, block:block + slots].astype(jnp.int32)
    row_class = jnp.arange(rows, dtype=jnp.int32) ^ r
    row_ids = jnp.arange(per_row, dtype=jnp.int32)[None, :] * rows + row_class[:, None]
    valid = slot_ids < total
    slot_snode = look_up(snode_of_block, slot_ids)
    slot_level = look_up(levels, slot_ids)
    row_snode = look_up(snode_of_block, row_ids)[..., None]
    row_level = look_up(levels, row_ids)[..., None]
    before = jnp.where(op == 0, row_ids[..., None] - slot_ids, slot_ids - row_ids[..., None]) > 0
    active = valid & jnp.where(slot_snode == row_snode, before, row_level > slot_level)
    table = jnp.where(active, slot_ids // cols, locals_here).reshape(-1)

    own_k = (c + cols * jnp.arange(groups, dtype=jnp.int32)) ^ r
    own_small = jnp.take(small, own_k, axis=0)
    own_ids = jnp.arange(per_row, dtype=jnp.int32)[None, :] * rows + c + cols * jnp.arange(groups)[:, None]
    own_slots = own_small[:, :, block:block + slots].astype(jnp.int32)
    slot_of = jnp.sum(
        jnp.where(own_slots == own_ids[..., None], jnp.arange(slots, dtype=jnp.int32), 0), axis=-1
    ).reshape(-1)

    def lay(values):
        shape = (per_row, groups, kept, block)
        return jnp.broadcast_to(values.transpose(1, 0, 2)[:, :, None], shape).reshape(-1, block)

    pivot = lay(jnp.where(op == 0, 1.0, own_small[:, :, :block]))
    level = lay(jnp.broadcast_to(look_up(levels, own_ids)[..., None], (groups, per_row, block)))

    step_ids = jnp.arange(steps, dtype=jnp.int32)
    at = jnp.sum((levels[None, :] == step_ids[:, None]).astype(jnp.int32), axis=1)
    upto = jnp.sum((levels[None, :] <= step_ids[:, None]).astype(jnp.int32), axis=1)
    solve_low = jnp.where(op == 0, upto - at, total - upto)
    solve_high = solve_low + at
    update_low = jnp.where(op == 0, upto, 0)
    update_high = jnp.where(op == 0, total, total - upto)
    bounds = jnp.stack(
        [
            solve_low // rows,
            (solve_high + rows - 1) // rows,
            update_low // rows,
            (update_high + rows - 1) // rows,
        ],
        axis=1,
    ).reshape(-1)
    scalars = jnp.concatenate([jnp.stack([(r % cols) ^ c, r // cols, op]), bounds]).astype(jnp.int32)

    chosen = jnp.where(op == 0, lower_rhs, upper_rhs)
    chosen = lax.dynamic_slice_in_dim(chosen, (r // 2) * kept, kept, 0)
    chosen = chosen.reshape(kept, per_row, groups, block).transpose(1, 2, 0, 3).reshape(-1, block)

    diag = prepare_diagonal((scalars, slot_of), dims, parts)
    run = functools.partial(
        step_kernel,
        dims=dims + (kept,),
        scalars=scalars,
        table=table,
        parts=parts,
        diag=diag,
        level=level,
        pivot=pivot,
    )

    def exchange(sends):
        return [sends[0]] + [xor_permute(sends[d], "col", d) for d in range(1, cols)]

    res = chosen
    sol = jnp.zeros(chosen.shape, jnp.float32)
    *sends, res = run("first", 0, state=(res, sol), received=[])
    for step in range(steps - 1):
        *sends, sol = run("solved", step, state=(res, sol), received=exchange(sends))
        *sends, res = run("updated", step, state=(res, sol), received=exchange(sends))
    sol = run("last", steps - 1, state=(res, sol), received=exchange(sends))

    whole = jnp.stack([sol] + [xor_permute(sol, "col", d) for d in range(1, cols)])
    for bit in bits_of(cols):
        paired = whole.reshape(cols // (2 * bit), 2, bit, *sol.shape)
        whole = jnp.where((c & bit) != 0, paired[:, ::-1], paired).reshape(cols, *sol.shape)
    whole = whole.reshape(cols, per_row, groups, kept, block).transpose(2, 0, 1, 3, 4)
    whole = whole.reshape(rows, per_row * kept, block)
    got = lax.all_to_all(whole, "row", 0, 0).reshape(rows // 2, 2, per_row, kept, block)
    got = got.transpose(1, 0, 3, 2, 4).reshape(2, rhs_count, per_row, block)
    return got[0], got[1]


def solution(mesh):
    in_specs = (
        P("row", "col", None, None),
        P("row", None),
        P(None, "col", None),
        P(None, "col", None),
        P(),
        P(),
        P("row", "col"),
    )
    out_specs = (P(None, "row", None), P(None, "row", None))
    return jax.shard_map(shards, mesh=mesh, in_specs=in_specs, out_specs=out_specs, check_vma=False)
```

```python
import functools

import jax
import jax.numpy as jnp
from jax import lax
from jax.experimental import pallas as pl
from jax.experimental.pallas import tpu as pltpu
from jax.sharding import PartitionSpec as P


def xor_permute(value, axis, distance):
    size = lax.axis_size(axis)
    return lax.ppermute(value, axis, [(i, i ^ distance) for i in range(size)])


def bits_of(size):
    return [1 << b for b in range(size.bit_length() - 1)]


def flip_order(values, position):
    size = values.shape[0]
    rest = values.shape[1:]
    for bit in bits_of(size):
        paired = values.reshape(size // (2 * bit), 2, bit, *rest)
        values = jnp.where((position & bit) != 0, paired[:, ::-1], paired).reshape(size, *rest)
    return values


def gather_rows(factor):
    size = lax.axis_size("row")
    half = factor.shape[0] // 2
    pieces = {0: (factor[:half], factor[half:])}
    for k in range(2, size, 2):
        high = 1 << (k.bit_length() - 1)
        low = k & -k
        pieces[k] = (
            xor_permute(pieces[k ^ high][0], "row", high),
            xor_permute(pieces[k ^ low][1], "row", low),
        )
    for k in range(0, size, 2):
        pieces[k ^ 1] = tuple(xor_permute(part, "row", 1) for part in pieces[k])
    return [part for k in range(size) for part in pieces[k]]


def vmem_budget(parts):
    return sum(part.size * part.dtype.itemsize for part in parts) * 5 // 4 + (2 << 20)


def load_operator(scalars, slot_of, dims, parts):
    rows, cols, groups, per_row, slots, block = dims
    half = per_row // 2

    def body(*refs):
        sc, slots_own = refs[0], refs[1]
        part_refs = refs[2:2 + 2 * rows]
        whole, diag, sems = refs[2 + 2 * rows:]
        row = sc[0]
        col = sc[1]
        op = sc[2]
        copies = []
        for k in range(rows):
            for h in range(2):
                copies.append(
                    pltpu.make_async_copy(
                        part_refs[2 * k + h], whole.at[pl.ds(h * half, half), row ^ k], sems.at[2 * k + h]
                    )
                )
                copies[-1].start()
        for copy in copies:
            copy.wait()
        row_i = lax.broadcasted_iota(jnp.int32, (block, block), 0)
        col_i = lax.broadcasted_iota(jnp.int32, (block, block), 1)
        ahead = jnp.where(op == 0, row_i - col_i, col_i - row_i) > 0
        for m in range(groups):
            for i in range(per_row):
                value = whole[i, col + cols * m, slots_own[m * per_row + i]].astype(jnp.float32)
                diag[m, i] = jnp.where(ahead, value, 0.0).astype(diag.dtype)

    vmem = pl.BlockSpec(memory_space=pltpu.VMEM)
    smem = pl.BlockSpec(memory_space=pltpu.SMEM)
    return pl.pallas_call(
        body,
        out_shape=[
            jax.ShapeDtypeStruct((per_row, rows, slots, block, block), parts[0].dtype),
            jax.ShapeDtypeStruct((groups, per_row, block, block), parts[0].dtype),
        ],
        in_specs=[smem, smem] + [pl.BlockSpec(memory_space=pl.ANY)] * len(parts),
        out_specs=[vmem, vmem],
        scratch_shapes=[pltpu.SemaphoreType.DMA((len(parts),))],
        compiler_params=pltpu.CompilerParams(vmem_limit_bytes=vmem_budget(parts)),
        name="load_operator",
    )(scalars, slot_of, *parts)


def step_kernel(kind, step, dims, scalars, table, operator, level, pivot, state, received):
    rows, cols, groups, per_row, slots, block, kept = dims
    lanes = groups * kept
    locals_here = per_row * groups
    flat = (per_row * lanes, block)
    tile = (per_row, lanes, block)

    def body(*refs):
        refs = list(refs)
        sc = refs.pop(0)
        idx = refs.pop(0)
        if kind != "last":
            whole = refs.pop(0)
            diag = refs.pop(0)
        level_ref = refs.pop(0)
        pivot_ref = refs.pop(0)
        res_ref = refs.pop(0)
        sol_ref = refs.pop(0)
        got = [refs.pop(0) for _ in received]
        if kind == "last":
            out_sol = refs.pop(0)
        else:
            sends = [refs.pop(0) for _ in range(cols)]
            out_state = refs.pop(0)
            xs, acc = refs
        lv = level_ref[...]
        res = res_ref[...]
        if got:
            total = got[0][...]
            for ref in got[1:]:
                total = total + ref[...].astype(jnp.float32)
        if kind in ("solved", "last"):
            rounded = res.astype(jnp.bfloat16).astype(jnp.float32)
            y = jnp.where(lv == step, total + pivot_ref[...] * rounded, 0.0)
            sol = sol_ref[...] + y
            if kind == "last":
                out_sol[...] = sol
                return
            out_state[...] = sol
            source = y
        elif kind == "updated":
            back = total.astype(jnp.bfloat16).astype(jnp.float32)
            res = jnp.where(lv > step, res - back, res)
            out_state[...] = res
            source = jnp.where(lv == step + 1, res, 0.0)
        else:
            out_state[...] = res
            source = jnp.where(lv == 0, res, 0.0)
        source = source.reshape(tile)
        lane_group = lax.broadcasted_iota(jnp.int32, (1, lanes, block), 1) // kept
        for shift in range(groups):
            moved = source
            if shift:
                moved = jnp.concatenate([source[:, lanes - shift * kept:], source[:, :lanes - shift * kept]], axis=1)
            for m in range(groups):
                mine = (m + groups - shift) % groups
                put = jnp.where(lane_group == m, moved, 0.0)
                for i in range(per_row):
                    xs[m, i * groups + mine] = put[i]
        for m in range(groups):
            xs[m, locals_here] = jnp.zeros((lanes, block), jnp.float32)
        acc[...] = jnp.zeros(acc.shape, jnp.float32)
        col = sc[1]
        which = 3 + 4 * (step + (1 if kind == "updated" else 0)) + (2 if kind == "solved" else 0)

        def contract(x, w):
            return lax.dot_general(
                x.astype(jnp.bfloat16), w, (((1,), (1,)), ((), ())), preferred_element_type=jnp.float32
            )

        def group(i, carry):
            for cc in range(cols):
                value = None
                for m in range(groups):
                    k = cc + cols * m
                    for s in range(slots):
                        j = idx[(i * rows + k) * slots + s]
                        term = contract(xs[m, j], whole[i, k, s])
                        value = term if value is None else value + term
                acc[cc, i] = value
            own = acc[col, i]
            for m in range(groups):
                own = own + contract(xs[m, i * groups + m], diag[m, i])
            acc[col, i] = own
            return carry

        lax.fori_loop(sc[which], sc[which + 1], group, 0)
        for d in range(cols):
            sends[d][...] = acc[col ^ d].reshape(flat).astype(sends[d].dtype)

    vmem = pl.BlockSpec(memory_space=pltpu.VMEM)
    smem = pl.BlockSpec(memory_space=pltpu.SMEM)
    budget = vmem_budget(operator)
    args = [scalars, table] + ([] if kind == "last" else list(operator)) + [level, pivot, *state, *received]
    if kind == "last":
        out_shape = jax.ShapeDtypeStruct(flat, jnp.float32)
        out_specs = vmem
        scratch = []
    else:
        out_shape = (
            [jax.ShapeDtypeStruct(flat, jnp.float32)]
            + [jax.ShapeDtypeStruct(flat, jnp.bfloat16)] * (cols - 1)
            + [jax.ShapeDtypeStruct(flat, jnp.float32)]
        )
        out_specs = [vmem] * (cols + 1)
        scratch = [
            pltpu.VMEM((groups, locals_here + 1, lanes, block), jnp.float32),
            pltpu.VMEM((cols, per_row, lanes, block), jnp.float32),
        ]
    return pl.pallas_call(
        body,
        out_shape=out_shape,
        in_specs=[smem, smem] + [vmem] * (len(args) - 2),
        out_specs=out_specs,
        scratch_shapes=scratch,
        compiler_params=pltpu.CompilerParams(vmem_limit_bytes=budget),
        name="step_" + kind,
    )(*args)


def shards(
    factor, inverse_pivot, lower_rhs, upper_rhs, snode_of_block, level_of_snode, slot_columns
):
    rows = lax.axis_size("row")
    cols = lax.axis_size("col")
    r = lax.axis_index("row")
    c = lax.axis_index("col")
    per_row, slots, block = factor.shape[:3]
    total = snode_of_block.shape[0]
    snodes = level_of_snode.shape[0]
    rhs_count = lower_rhs.shape[0]
    steps = min(6, snodes // 2)
    groups = rows // cols
    kept = 2 * rhs_count // rows
    locals_here = per_row * groups
    lanes = groups * kept
    op = r % 2
    dims = (rows, cols, groups, per_row, slots, block)

    small = jnp.concatenate(
        [inverse_pivot, jnp.pad(slot_columns.astype(jnp.float32), ((0, 0), (0, block - slots)))], axis=1
    )[None]
    for bit in bits_of(rows):
        small = jnp.concatenate([small, xor_permute(small, "row", bit)], axis=0)
    parts = gather_rows(factor)

    blocks = jnp.arange(total, dtype=jnp.int32)
    onehot = snode_of_block[:, None] == jnp.arange(snodes, dtype=jnp.int32)[None, :]
    levels = jnp.sum(jnp.where(onehot, level_of_snode[None, :], 0), axis=1)
    levels = jnp.where(op == 0, levels, steps - 1 - levels)

    def look_up(values, index):
        return jnp.sum(jnp.where(index[..., None] == blocks, values, 0), axis=-1)

    small = flip_order(small, r)
    slot_ids = small[:, :, block:block + slots].astype(jnp.int32).transpose(1, 0, 2)
    row_ids = blocks.reshape(per_row, rows)
    valid = slot_ids < total
    slot_snode = look_up(snode_of_block, slot_ids)
    slot_level = look_up(levels, slot_ids)
    row_snode = look_up(snode_of_block, row_ids)[..., None]
    row_level = look_up(levels, row_ids)[..., None]
    before = jnp.where(op == 0, row_ids[..., None] - slot_ids, slot_ids - row_ids[..., None]) > 0
    active = valid & jnp.where(slot_snode == row_snode, before, row_level > slot_level)
    table = jnp.where(active, slot_ids // cols, locals_here).reshape(-1)

    own_small = lax.dynamic_index_in_dim(small.reshape(groups, cols, *small.shape[1:]), c, 1, keepdims=False)
    own_ids = jnp.arange(per_row, dtype=jnp.int32)[None, :] * rows + c + cols * jnp.arange(groups)[:, None]
    own_slots = own_small[:, :, block:block + slots].astype(jnp.int32)
    slot_of = jnp.sum(
        jnp.where(own_slots == own_ids[..., None], jnp.arange(slots, dtype=jnp.int32), 0), axis=-1
    ).reshape(-1)

    def lay(values):
        shape = (per_row, groups, kept, block)
        return jnp.broadcast_to(values.transpose(1, 0, 2)[:, :, None], shape).reshape(-1, block)

    pivot = lay(jnp.where(op == 0, 1.0, own_small[:, :, :block]))
    level = lay(jnp.broadcast_to(look_up(levels, own_ids)[..., None], (groups, per_row, block)))

    step_ids = jnp.arange(steps, dtype=jnp.int32)
    at = jnp.sum((levels[None, :] == step_ids[:, None]).astype(jnp.int32), axis=1)
    upto = jnp.sum((levels[None, :] <= step_ids[:, None]).astype(jnp.int32), axis=1)
    solve_low = jnp.where(op == 0, upto - at, total - upto)
    solve_high = solve_low + at
    update_low = jnp.where(op == 0, upto, 0)
    update_high = jnp.where(op == 0, total, total - upto)
    bounds = jnp.stack(
        [
            solve_low // rows,
            (solve_high + rows - 1) // rows,
            update_low // rows,
            (update_high + rows - 1) // rows,
        ],
        axis=1,
    ).reshape(-1)
    scalars = jnp.concatenate([jnp.stack([r, c, op]), bounds]).astype(jnp.int32)

    chosen = jnp.where(op == 0, lower_rhs, upper_rhs)
    chosen = lax.dynamic_slice_in_dim(chosen, (r // 2) * kept, kept, 0)
    chosen = chosen.reshape(kept, per_row, groups, block).transpose(1, 2, 0, 3).reshape(-1, block)

    operator = load_operator(scalars, slot_of, dims, parts)
    run = functools.partial(
        step_kernel,
        dims=dims + (kept,),
        scalars=scalars,
        table=table,
        operator=operator,
        level=level,
        pivot=pivot,
    )

    def exchange(sends):
        return [sends[0]] + [xor_permute(sends[d], "col", d) for d in range(1, cols)]

    res = chosen
    sol = jnp.zeros(chosen.shape, jnp.float32)
    *sends, res = run("first", 0, state=(res, sol), received=[])
    for step in range(steps - 1):
        *sends, sol = run("solved", step, state=(res, sol), received=exchange(sends))
        *sends, res = run("updated", step, state=(res, sol), received=exchange(sends))
    sol = run("last", steps - 1, state=(res, sol), received=exchange(sends))

    whole = jnp.stack([sol] + [xor_permute(sol, "col", d) for d in range(1, cols)])
    whole = flip_order(whole, c)
    whole = whole.reshape(cols, per_row, groups, kept, block).transpose(2, 0, 1, 3, 4)
    whole = whole.reshape(rows, per_row * kept, block)
    got = lax.all_to_all(whole, "row", 0, 0).reshape(rows // 2, 2, per_row, kept, block)
    got = got.transpose(1, 0, 3, 2, 4).reshape(2, rhs_count, per_row, block)
    return got[0], got[1]


def solution(mesh):
    in_specs = (
        P("row", "col", None, None),
        P("row", None),
        P(None, "col", None),
        P(None, "col", None),
        P(),
        P(),
        P("row", "col"),
    )
    out_specs = (P(None, "row", None), P(None, "row", None))
    return jax.shard_map(shards, mesh=mesh, in_specs=in_specs, out_specs=out_specs, check_vma=False)
```

```python
import functools

import jax
import jax.numpy as jnp
from jax import lax
from jax.experimental import pallas as pl
from jax.experimental.pallas import tpu as pltpu
from jax.sharding import PartitionSpec as P


def xor_permute(value, axis, distance):
    size = lax.axis_size(axis)
    return lax.ppermute(value, axis, [(i, i ^ distance) for i in range(size)])


def bits_of(size):
    return [1 << b for b in range(size.bit_length() - 1)]


def flip_order(values, position):
    size = values.shape[0]
    rest = values.shape[1:]
    for bit in bits_of(size):
        paired = values.reshape(size // (2 * bit), 2, bit, *rest)
        values = jnp.where((position & bit) != 0, paired[:, ::-1], paired).reshape(size, *rest)
    return values


def gather_rows(factor, small):
    size = lax.axis_size("row")
    half = factor.shape[0] // 2

    def move(value, distance):
        return xor_permute(value, "row", distance)

    tables = jnp.stack([small] + [move(small, k) for k in range(2, size, 2)])
    pieces = {0: (factor[:half], factor[half:])}
    for k in range(2, size, 2):
        high = 1 << (k.bit_length() - 1)
        low = k & -k
        pieces[k] = (move(pieces[k ^ high][0], high), move(pieces[k ^ low][1], low))
    for k in range(0, size, 2):
        pieces[k ^ 1] = tuple(move(part, 1) for part in pieces[k])
    tables = jnp.stack([tables, move(tables, 1)], axis=1).reshape(size, *small.shape)
    return [part for k in range(size) for part in pieces[k]], tables


def vmem_budget(parts):
    return sum(part.size * part.dtype.itemsize for part in parts) * 5 // 4 + (2 << 20)


def load_operator(scalars, slot_of, dims, parts):
    rows, cols, groups, per_row, slots, block = dims
    half = per_row // 2

    def body(*refs):
        sc, slots_own = refs[0], refs[1]
        part_refs = refs[2:2 + 2 * rows]
        whole, diag, sems = refs[2 + 2 * rows:]
        row = sc[0]
        col = sc[1]
        op = sc[2]
        copies = []
        for k in range(rows):
            for h in range(2):
                copies.append(
                    pltpu.make_async_copy(
                        part_refs[2 * k + h], whole.at[pl.ds(h * half, half), row ^ k], sems.at[2 * k + h]
                    )
                )
                copies[-1].start()
        for copy in copies:
            copy.wait()
        row_i = lax.broadcasted_iota(jnp.int32, (block, block), 0)
        col_i = lax.broadcasted_iota(jnp.int32, (block, block), 1)
        ahead = jnp.where(op == 0, row_i - col_i, col_i - row_i) > 0
        for m in range(groups):
            for i in range(per_row):
                value = whole[i, col + cols * m, slots_own[m * per_row + i]].astype(jnp.float32)
                diag[m, i] = jnp.where(ahead, value, 0.0).astype(diag.dtype)

    vmem = pl.BlockSpec(memory_space=pltpu.VMEM)
    smem = pl.BlockSpec(memory_space=pltpu.SMEM)
    return pl.pallas_call(
        body,
        out_shape=[
            jax.ShapeDtypeStruct((per_row, rows, slots, block, block), parts[0].dtype),
            jax.ShapeDtypeStruct((groups, per_row, block, block), parts[0].dtype),
        ],
        in_specs=[smem, smem] + [pl.BlockSpec(memory_space=pl.ANY)] * len(parts),
        out_specs=[vmem, vmem],
        scratch_shapes=[pltpu.SemaphoreType.DMA((len(parts),))],
        compiler_params=pltpu.CompilerParams(vmem_limit_bytes=vmem_budget(parts)),
        name="load_operator",
    )(scalars, slot_of, *parts)


def step_kernel(kind, step, dims, scalars, table, operator, level, pivot, state, received):
    rows, cols, groups, per_row, slots, block, kept = dims
    lanes = groups * kept
    locals_here = per_row * groups
    flat = (per_row * lanes, block)
    tile = (per_row, lanes, block)

    def body(*refs):
        refs = list(refs)
        sc = refs.pop(0)
        idx = refs.pop(0)
        if kind != "last":
            whole = refs.pop(0)
            diag = refs.pop(0)
        level_ref = refs.pop(0)
        pivot_ref = refs.pop(0)
        res_ref = refs.pop(0)
        sol_ref = refs.pop(0)
        got = [refs.pop(0) for _ in received]
        if kind == "last":
            out_sol = refs.pop(0)
        else:
            sends = [refs.pop(0) for _ in range(cols)]
            out_state = refs.pop(0)
            xs, acc = refs
        lv = level_ref[...]
        res = res_ref[...]
        if got:
            total = got[0][...]
            for ref in got[1:]:
                total = total + ref[...].astype(jnp.float32)
        if kind in ("solved", "last"):
            rounded = res.astype(jnp.bfloat16).astype(jnp.float32)
            y = jnp.where(lv == step, total + pivot_ref[...] * rounded, 0.0)
            sol = sol_ref[...] + y
            if kind == "last":
                out_sol[...] = sol
                return
            out_state[...] = sol
            source = y
        elif kind == "updated":
            back = total.astype(jnp.bfloat16).astype(jnp.float32)
            res = jnp.where(lv > step, res - back, res)
            out_state[...] = res
            source = jnp.where(lv == step + 1, res, 0.0)
        else:
            out_state[...] = res
            source = jnp.where(lv == 0, res, 0.0)
        source = source.reshape(tile)
        lane_group = lax.broadcasted_iota(jnp.int32, (1, lanes, block), 1) // kept
        for shift in range(groups):
            moved = source
            if shift:
                moved = jnp.concatenate([source[:, lanes - shift * kept:], source[:, :lanes - shift * kept]], axis=1)
            for m in range(groups):
                mine = (m + groups - shift) % groups
                put = jnp.where(lane_group == m, moved, 0.0)
                for i in range(per_row):
                    xs[m, i * groups + mine] = put[i]
        for m in range(groups):
            xs[m, locals_here] = jnp.zeros((lanes, block), jnp.float32)
        acc[...] = jnp.zeros(acc.shape, jnp.float32)
        col = sc[1]
        which = 3 + 4 * (step + (1 if kind == "updated" else 0)) + (2 if kind == "solved" else 0)

        def contract(x, w):
            return lax.dot_general(
                x.astype(jnp.bfloat16), w, (((1,), (1,)), ((), ())), preferred_element_type=jnp.float32
            )

        def group(i, carry):
            for cc in range(cols):
                left = []
                right = []
                for m in range(groups):
                    k = cc + cols * m
                    for s in range(slots):
                        left.append(xs[m, idx[(i * rows + k) * slots + s]])
                        right.append(whole[i, k, s])
                acc[cc, i] = contract(jnp.concatenate(left, axis=1), jnp.concatenate(right, axis=1))
            left = [xs[m, i * groups + m] for m in range(groups)]
            right = [diag[m, i] for m in range(groups)]
            acc[col, i] += contract(jnp.concatenate(left, axis=1), jnp.concatenate(right, axis=1))
            return carry

        lax.fori_loop(sc[which], sc[which + 1], group, 0)
        for d in range(cols):
            sends[d][...] = acc[col ^ d].reshape(flat).astype(sends[d].dtype)

    vmem = pl.BlockSpec(memory_space=pltpu.VMEM)
    smem = pl.BlockSpec(memory_space=pltpu.SMEM)
    budget = vmem_budget(operator)
    args = [scalars, table] + ([] if kind == "last" else list(operator)) + [level, pivot, *state, *received]
    if kind == "last":
        out_shape = jax.ShapeDtypeStruct(flat, jnp.float32)
        out_specs = vmem
        scratch = []
    else:
        out_shape = (
            [jax.ShapeDtypeStruct(flat, jnp.float32)]
            + [jax.ShapeDtypeStruct(flat, jnp.bfloat16)] * (cols - 1)
            + [jax.ShapeDtypeStruct(flat, jnp.float32)]
        )
        out_specs = [vmem] * (cols + 1)
        scratch = [
            pltpu.VMEM((groups, locals_here + 1, lanes, block), jnp.float32),
            pltpu.VMEM((cols, per_row, lanes, block), jnp.float32),
        ]
    return pl.pallas_call(
        body,
        out_shape=out_shape,
        in_specs=[smem, smem] + [vmem] * (len(args) - 2),
        out_specs=out_specs,
        scratch_shapes=scratch,
        compiler_params=pltpu.CompilerParams(vmem_limit_bytes=budget),
    )(*args)


def shards(
    factor, inverse_pivot, lower_rhs, upper_rhs, snode_of_block, level_of_snode, slot_columns
):
    rows = lax.axis_size("row")
    cols = lax.axis_size("col")
    r = lax.axis_index("row")
    c = lax.axis_index("col")
    per_row, slots, block = factor.shape[:3]
    total = snode_of_block.shape[0]
    snodes = level_of_snode.shape[0]
    rhs_count = lower_rhs.shape[0]
    steps = min(6, snodes // 2)
    groups = rows // cols
    kept = 2 * rhs_count // rows
    locals_here = per_row * groups
    op = r % 2
    dims = (rows, cols, groups, per_row, slots, block)

    small = jnp.concatenate(
        [inverse_pivot, jnp.pad(slot_columns.astype(jnp.float32), ((0, 0), (0, block - slots)))], axis=1
    )
    parts, small = gather_rows(factor, small)

    blocks = jnp.arange(total, dtype=jnp.int32)
    onehot = snode_of_block[:, None] == jnp.arange(snodes, dtype=jnp.int32)[None, :]
    levels = jnp.sum(jnp.where(onehot, level_of_snode[None, :], 0), axis=1)
    levels = jnp.where(op == 0, levels, steps - 1 - levels)

    def look_up(values, index):
        return jnp.sum(jnp.where(index[..., None] == blocks, values, 0), axis=-1)

    small = flip_order(small, r)
    slot_ids = small[:, :, block:block + slots].astype(jnp.int32).transpose(1, 0, 2)
    row_ids = blocks.reshape(per_row, rows)
    valid = slot_ids < total
    slot_snode = look_up(snode_of_block, slot_ids)
    slot_level = look_up(levels, slot_ids)
    row_snode = look_up(snode_of_block, row_ids)[..., None]
    row_level = look_up(levels, row_ids)[..., None]
    before = jnp.where(op == 0, row_ids[..., None] - slot_ids, slot_ids - row_ids[..., None]) > 0
    active = valid & jnp.where(slot_snode == row_snode, before, row_level > slot_level)
    table = jnp.where(active, slot_ids // cols, locals_here).reshape(-1)

    own_small = lax.dynamic_index_in_dim(small.reshape(groups, cols, *small.shape[1:]), c, 1, keepdims=False)
    own_ids = jnp.arange(per_row, dtype=jnp.int32)[None, :] * rows + c + cols * jnp.arange(groups)[:, None]
    own_slots = own_small[:, :, block:block + slots].astype(jnp.int32)
    slot_of = jnp.sum(
        jnp.where(own_slots == own_ids[..., None], jnp.arange(slots, dtype=jnp.int32), 0), axis=-1
    ).reshape(-1)

    def lay(values):
        shape = (per_row, groups, kept, block)
        return jnp.broadcast_to(values.transpose(1, 0, 2)[:, :, None], shape).reshape(-1, block)

    pivot = lay(jnp.where(op == 0, 1.0, own_small[:, :, :block]))
    level = lay(jnp.broadcast_to(look_up(levels, own_ids)[..., None], (groups, per_row, block)))

    step_ids = jnp.arange(steps, dtype=jnp.int32)
    at = jnp.sum((levels[None, :] == step_ids[:, None]).astype(jnp.int32), axis=1)
    upto = jnp.sum((levels[None, :] <= step_ids[:, None]).astype(jnp.int32), axis=1)
    solve_low = jnp.where(op == 0, upto - at, total - upto)
    solve_high = solve_low + at
    update_low = jnp.where(op == 0, upto, 0)
    update_high = jnp.where(op == 0, total, total - upto)
    bounds = jnp.stack(
        [
            solve_low // rows,
            (solve_high + rows - 1) // rows,
            update_low // rows,
            (update_high + rows - 1) // rows,
        ],
        axis=1,
    ).reshape(-1)
    scalars = jnp.concatenate([jnp.stack([r, c, op]), bounds]).astype(jnp.int32)

    chosen = jnp.where(op == 0, lower_rhs, upper_rhs)
    chosen = lax.dynamic_slice_in_dim(chosen, (r // 2) * kept, kept, 0)
    chosen = chosen.reshape(kept, per_row, groups, block).transpose(1, 2, 0, 3).reshape(-1, block)

    operator = load_operator(scalars, slot_of, dims, parts)
    run = functools.partial(
        step_kernel,
        dims=dims + (kept,),
        scalars=scalars,
        table=table,
        operator=operator,
        level=level,
        pivot=pivot,
    )

    def exchange(sends):
        got = [sends[0]]
        for d in range(1, cols):
            got.append(xor_permute(sends[d], "col", d))
        return got

    res = chosen
    sol = jnp.zeros(chosen.shape, jnp.float32)
    *sends, res = run("first", 0, state=(res, sol), received=[])
    for step in range(steps - 1):
        *sends, sol = run("solved", step, state=(res, sol), received=exchange(sends))
        *sends, res = run("updated", step, state=(res, sol), received=exchange(sends))
    sol = run("last", steps - 1, state=(res, sol), received=exchange(sends))

    whole = jnp.stack(exchange([sol] * cols))
    whole = flip_order(whole, c)
    whole = whole.reshape(cols, per_row, groups, kept, block).transpose(2, 0, 1, 3, 4)
    whole = whole.reshape(rows, per_row * kept, block)
    got = lax.all_to_all(whole, "row", 0, 0).reshape(rows // 2, 2, per_row, kept, block)
    got = got.transpose(1, 0, 3, 2, 4).reshape(2, rhs_count, per_row, block)
    return got[0], got[1]


def solution(mesh):
    in_specs = (
        P("row", "col", None, None),
        P("row", None),
        P(None, "col", None),
        P(None, "col", None),
        P(),
        P(),
        P("row", "col"),
    )
    out_specs = (P(None, "row", None), P(None, "row", None))
    return jax.shard_map(shards, mesh=mesh, in_specs=in_specs, out_specs=out_specs, check_vma=False)
```

```python
import functools
import math

import jax
import jax.numpy as jnp
from jax import lax
from jax.experimental import pallas as pl
from jax.experimental.pallas import tpu as pltpu
from jax.sharding import PartitionSpec as P


def xor_permute(value, axis, distance):
    size = lax.axis_size(axis)
    return lax.ppermute(value, axis, [(i, i ^ distance) for i in range(size)])


def bits_of(size):
    return [1 << b for b in range(size.bit_length() - 1)]


def flip_order(values, position):
    size = values.shape[0]
    rest = values.shape[1:]
    for bit in bits_of(size):
        paired = values.reshape(size // (2 * bit), 2, bit, *rest)
        values = jnp.where((position & bit) != 0, paired[:, ::-1], paired).reshape(size, *rest)
    return values


def gather_rows(factor, small):
    size = lax.axis_size("row")
    half = factor.shape[0] // 2

    def move(value, distance):
        return xor_permute(value, "row", distance)

    tables = jnp.stack([small] + [move(small, k) for k in range(2, size, 2)])
    pieces = {0: (factor[:half], factor[half:])}
    for k in range(2, size, 2):
        high = 1 << (k.bit_length() - 1)
        low = k & -k
        pieces[k] = (move(pieces[k ^ high][0], high), move(pieces[k ^ low][1], low))
    for k in range(0, size, 2):
        pieces[k ^ 1] = tuple(move(part, 1) for part in pieces[k])
    tables = jnp.stack([tables, move(tables, 1)], axis=1).reshape(size, *small.shape)
    return [part for k in range(size) for part in pieces[k]], tables


def vmem_budget(parts):
    return sum(part.size * part.dtype.itemsize for part in parts) * 5 // 4 + (2 << 20)


def load_blocks(scalars, slot_of, extras, dims, which, parts, whole, last):
    rows, cols, groups, per_row, slots, block = dims
    half = per_row // 2
    dtype = parts[0].dtype

    def body(*refs):
        sc, slots_own = refs[:2]
        part_refs = refs[2:2 + len(parts)]
        outs = refs[len(args):]
        out = outs[0]
        row = sc[0]
        for n in range(len(parts)):
            def move(i, carry, n=n):
                for s in range(slots):
                    out[n % 2 * half + i, row ^ which[n // 2], s] = part_refs[n][i, s].T
                return carry

            lax.fori_loop(0, half, move, 0, unroll=2)
        if last:
            diag = outs[1]
            col = sc[1]
            op = sc[2]
            row_i = lax.broadcasted_iota(jnp.int32, (block, block), 0)
            col_i = lax.broadcasted_iota(jnp.int32, (block, block), 1)
            ahead = jnp.where(op == 0, col_i - row_i, row_i - col_i) > 0
            for m in range(groups):
                for i in range(per_row):
                    value = out[i, col + cols * m, slots_own[m * per_row + i]].astype(jnp.float32)
                    diag[m, i] = jnp.where(ahead, value, 0.0).astype(dtype)

    vmem = pl.BlockSpec(memory_space=pltpu.VMEM)
    smem = pl.BlockSpec(memory_space=pltpu.SMEM)
    hbm = pl.BlockSpec(memory_space=pl.ANY)
    args = [scalars, slot_of, *parts, *extras] + ([] if whole is None else [whole])
    shapes = [jax.ShapeDtypeStruct((per_row, rows, slots, block, block), dtype)]
    if last:
        shapes.append(jax.ShapeDtypeStruct((groups, per_row, block, block), dtype))
    need = sum(math.prod(shape.shape) for shape in shapes) + sum(part.size for part in parts)
    return pl.pallas_call(
        body,
        out_shape=shapes,
        in_specs=[smem] * 2 + [vmem] * len(parts) + [hbm] * (len(args) - 2 - len(parts)),
        out_specs=[vmem] * len(shapes),
        input_output_aliases={} if whole is None else {len(args) - 1: 0},
        compiler_params=pltpu.CompilerParams(vmem_limit_bytes=need * dtype.itemsize + (2 << 20)),
        name="load_blocks",
    )(*args)


def load_operator(scalars, slot_of, extras, dims, parts):
    early = [k for k in range(dims[0]) if (k >> 1) & ((k >> 1) - 1) == 0]
    late = [k for k in range(dims[0]) if k not in early]
    stages = [which for which in (early, late) if which]
    loaded = [None]
    for n, which in enumerate(stages):
        chosen = [part for k in which for part in parts[2 * k:2 * k + 2]]
        loaded = load_blocks(
            scalars, slot_of, extras if n == 0 else [], dims, which, chosen, loaded[0], n + 1 == len(stages)
        )
    return loaded


def step_kernel(kind, step, dims, scalars, table, operator, level, pivot, state, received):
    rows, cols, groups, per_row, slots, block, kept = dims
    lanes = groups * kept
    locals_here = per_row * groups
    flat = (per_row * lanes, block)
    tile = (per_row, lanes, block)

    def body(*refs):
        refs = list(refs)
        sc = refs.pop(0)
        idx = refs.pop(0)
        if kind != "last":
            whole = refs.pop(0)
            diag = refs.pop(0)
        level_ref = refs.pop(0)
        pivot_ref = refs.pop(0)
        res_ref = refs.pop(0)
        sol_ref = refs.pop(0) if len(state) > 1 else None
        got = [refs.pop(0) for _ in received]
        if kind == "last":
            out_sol = refs.pop(0)
        else:
            sends = [refs.pop(0) for _ in range(cols)]
            out_state = refs.pop(0)
            xs, acc = refs
        lv = level_ref[...]
        res = res_ref[...]
        if got:
            total = got[0][...]
            for ref in got[1:]:
                total = total + ref[...].astype(jnp.float32)
        if kind in ("solved", "last"):
            rounded = res.astype(jnp.bfloat16).astype(jnp.float32)
            y = jnp.where(lv == step, total + pivot_ref[...] * rounded, 0.0)
            sol = y if sol_ref is None else sol_ref[...] + y
            if kind == "last":
                out_sol[...] = sol
                return
            out_state[...] = sol
            source = y
        elif kind == "updated":
            back = total.astype(jnp.bfloat16).astype(jnp.float32)
            res = jnp.where(lv > step, res - back, res)
            out_state[...] = res
            source = jnp.where(lv == step + 1, res, 0.0)
        else:
            out_state[...] = res
            source = jnp.where(lv == 0, res, 0.0)
        source = source.reshape(tile)
        lane_group = lax.broadcasted_iota(jnp.int32, (1, lanes, block), 1) // kept
        for shift in range(groups):
            moved = source
            if shift:
                moved = jnp.concatenate([source[:, lanes - shift * kept:], source[:, :lanes - shift * kept]], axis=1)
            for m in range(groups):
                mine = (m + groups - shift) % groups
                put = jnp.where(lane_group == m, moved, 0.0)
                for i in range(per_row):
                    xs[m, i * groups + mine] = put[i]
        for m in range(groups):
            xs[m, locals_here] = jnp.zeros((lanes, block), jnp.float32)
        acc[...] = jnp.zeros(acc.shape, jnp.float32)
        col = sc[1]
        which = 3 + 4 * (step + (1 if kind == "updated" else 0)) + (2 if kind == "solved" else 0)

        def contract(x, w):
            return lax.dot_general(
                x.astype(jnp.bfloat16), w, (((1,), (0,)), ((), ())), preferred_element_type=jnp.float32
            )

        def group(i, carry):
            for cc in range(cols):
                left = []
                right = []
                for m in range(groups):
                    k = cc + cols * m
                    for s in range(slots):
                        left.append(xs[m, idx[(i * rows + k) * slots + s]])
                        right.append(whole[i, k, s])
                acc[cc, i] = contract(jnp.concatenate(left, axis=1), jnp.concatenate(right, axis=0))
            left = [xs[m, i * groups + m] for m in range(groups)]
            right = [diag[m, i] for m in range(groups)]
            acc[col, i] += contract(jnp.concatenate(left, axis=1), jnp.concatenate(right, axis=0))
            return carry

        lax.fori_loop(sc[which], sc[which + 1], group, 0)
        for d in range(cols):
            sends[d][...] = acc[col ^ d].reshape(flat).astype(sends[d].dtype)

    vmem = pl.BlockSpec(memory_space=pltpu.VMEM)
    smem = pl.BlockSpec(memory_space=pltpu.SMEM)
    budget = vmem_budget(operator)
    args = [scalars, table] + ([] if kind == "last" else list(operator)) + [level, pivot, *state, *received]
    if kind == "last":
        out_shape = jax.ShapeDtypeStruct(flat, jnp.float32)
        out_specs = vmem
        scratch = []
    else:
        out_shape = (
            [jax.ShapeDtypeStruct(flat, jnp.float32)]
            + [jax.ShapeDtypeStruct(flat, jnp.bfloat16)] * (cols - 1)
            + [jax.ShapeDtypeStruct(flat, jnp.float32)]
        )
        out_specs = [vmem] * (cols + 1)
        scratch = [
            pltpu.VMEM((groups, locals_here + 1, lanes, block), jnp.float32),
            pltpu.VMEM((cols, per_row, lanes, block), jnp.float32),
        ]
    return pl.pallas_call(
        body,
        out_shape=out_shape,
        in_specs=[smem, smem] + [vmem] * (len(args) - 2),
        out_specs=out_specs,
        scratch_shapes=scratch,
        compiler_params=pltpu.CompilerParams(vmem_limit_bytes=budget),
    )(*args)


def shards(
    factor, inverse_pivot, lower_rhs, upper_rhs, snode_of_block, level_of_snode, slot_columns
):
    rows = lax.axis_size("row")
    cols = lax.axis_size("col")
    r = lax.axis_index("row")
    c = lax.axis_index("col")
    per_row, slots, block = factor.shape[:3]
    total = snode_of_block.shape[0]
    snodes = level_of_snode.shape[0]
    rhs_count = lower_rhs.shape[0]
    steps = min(6, snodes // 2)
    groups = rows // cols
    kept = 2 * rhs_count // rows
    locals_here = per_row * groups
    op = r % 2
    dims = (rows, cols, groups, per_row, slots, block)

    small = jnp.concatenate(
        [inverse_pivot, jnp.pad(slot_columns.astype(jnp.float32), ((0, 0), (0, block - slots)))], axis=1
    )
    parts, small = gather_rows(factor, small)

    blocks = jnp.arange(total, dtype=jnp.int32)
    onehot = snode_of_block[:, None] == jnp.arange(snodes, dtype=jnp.int32)[None, :]
    levels = jnp.sum(jnp.where(onehot, level_of_snode[None, :], 0), axis=1)
    levels = jnp.where(op == 0, levels, steps - 1 - levels)

    def look_up(values, index):
        return jnp.sum(jnp.where(index[..., None] == blocks, values, 0), axis=-1)

    small = flip_order(small, r)
    slot_ids = small[:, :, block:block + slots].astype(jnp.int32).transpose(1, 0, 2)
    row_ids = blocks.reshape(per_row, rows)
    valid = slot_ids < total
    slot_snode = look_up(snode_of_block, slot_ids)
    slot_level = look_up(levels, slot_ids)
    row_snode = look_up(snode_of_block, row_ids)[..., None]
    row_level = look_up(levels, row_ids)[..., None]
    before = jnp.where(op == 0, row_ids[..., None] - slot_ids, slot_ids - row_ids[..., None]) > 0
    active = valid & jnp.where(slot_snode == row_snode, before, row_level > slot_level)
    table = jnp.where(active, slot_ids // cols, locals_here).reshape(-1)

    own_small = lax.dynamic_index_in_dim(small.reshape(groups, cols, *small.shape[1:]), c, 1, keepdims=False)
    own_ids = jnp.arange(per_row, dtype=jnp.int32)[None, :] * rows + c + cols * jnp.arange(groups)[:, None]
    own_slots = own_small[:, :, block:block + slots].astype(jnp.int32)
    slot_of = jnp.sum(
        jnp.where(own_slots == own_ids[..., None], jnp.arange(slots, dtype=jnp.int32), 0), axis=-1
    ).reshape(-1)

    def lay(values):
        shape = (per_row, groups, kept, block)
        return jnp.broadcast_to(values.transpose(1, 0, 2)[:, :, None], shape).reshape(-1, block)

    pivot = lay(jnp.where(op == 0, 1.0, own_small[:, :, :block]))
    level = lay(jnp.broadcast_to(look_up(levels, own_ids)[..., None], (groups, per_row, block)))

    step_ids = jnp.arange(steps, dtype=jnp.int32)
    at = jnp.sum((levels[None, :] == step_ids[:, None]).astype(jnp.int32), axis=1)
    upto = jnp.sum((levels[None, :] <= step_ids[:, None]).astype(jnp.int32), axis=1)
    solve_low = jnp.where(op == 0, upto - at, total - upto)
    solve_high = solve_low + at
    update_low = jnp.where(op == 0, upto, 0)
    update_high = jnp.where(op == 0, total, total - upto)
    bounds = jnp.stack(
        [
            solve_low // rows,
            (solve_high + rows - 1) // rows,
            update_low // rows,
            (update_high + rows - 1) // rows,
        ],
        axis=1,
    ).reshape(-1)
    scalars = jnp.concatenate([jnp.stack([r, c, op]), bounds]).astype(jnp.int32)

    chosen = jnp.where(op == 0, lower_rhs, upper_rhs)
    chosen = lax.dynamic_slice_in_dim(chosen, (r // 2) * kept, kept, 0)
    chosen = chosen.reshape(kept, per_row, groups, block).transpose(1, 2, 0, 3).reshape(-1, block)

    operator = load_operator(scalars, slot_of, [table, level, pivot, chosen], dims, parts)
    run = functools.partial(
        step_kernel,
        dims=dims + (kept,),
        scalars=scalars,
        table=table,
        operator=operator,
        level=level,
        pivot=pivot,
    )

    def exchange(sends):
        got = [sends[0]]
        for d in range(1, cols):
            got.append(xor_permute(sends[d], "col", d))
        return got

    res = chosen
    *sends, res = run("first", 0, state=(res,), received=[])
    for step in range(steps - 1):
        *sends, sol = run("solved", step, state=(res, sol) if step else (res,), received=exchange(sends))
        *sends, res = run("updated", step, state=(res,), received=exchange(sends))
    sol = run("last", steps - 1, state=(res, sol), received=exchange(sends))

    whole = jnp.stack(exchange([sol] * cols))
    whole = flip_order(whole, c)
    whole = whole.reshape(cols, per_row, groups, kept, block).transpose(2, 0, 1, 3, 4)
    whole = whole.reshape(rows, per_row * kept, block)
    got = lax.all_to_all(whole, "row", 0, 0).reshape(rows // 2, 2, per_row, kept, block)
    got = got.transpose(1, 0, 3, 2, 4).reshape(2, rhs_count, per_row, block)
    return got[0], got[1]


def solution(mesh):
    in_specs = (
        P("row", "col", None, None),
        P("row", None),
        P(None, "col", None),
        P(None, "col", None),
        P(),
        P(),
        P("row", "col"),
    )
    out_specs = (P(None, "row", None), P(None, "row", None))
    return jax.shard_map(shards, mesh=mesh, in_specs=in_specs, out_specs=out_specs, check_vma=False)
```

```python
import functools
import math

import jax
import jax.numpy as jnp
from jax import lax
from jax.experimental import pallas as pl
from jax.experimental.pallas import tpu as pltpu
from jax.sharding import PartitionSpec as P


def xor_permute(value, axis, distance):
    size = lax.axis_size(axis)
    return lax.ppermute(value, axis, [(i, i ^ distance) for i in range(size)])


def bits_of(size):
    return [1 << b for b in range(size.bit_length() - 1)]


def flip_order(values, position):
    size = values.shape[0]
    rest = values.shape[1:]
    for bit in bits_of(size):
        paired = values.reshape(size // (2 * bit), 2, bit, *rest)
        values = jnp.where((position & bit) != 0, paired[:, ::-1], paired).reshape(size, *rest)
    return values


def gather_rows(factor, small):
    size = lax.axis_size("row")
    half = factor.shape[0] // 2

    def move(value, distance):
        return xor_permute(value, "row", distance)

    tables = jnp.stack([small] + [move(small, k) for k in range(2, size, 2)])
    pieces = {0: (factor[:half], factor[half:])}
    for k in range(2, size, 2):
        high = 1 << (k.bit_length() - 1)
        low = k & -k
        pieces[k] = (move(pieces[k ^ high][0], high), move(pieces[k ^ low][1], low))
    for k in range(0, size, 2):
        pieces[k ^ 1] = tuple(move(part, 1) for part in pieces[k])
    tables = jnp.stack([tables, move(tables, 1)], axis=1).reshape(size, *small.shape)
    return [part for k in range(size) for part in pieces[k]], tables


def vmem_budget(parts):
    return sum(part.size * part.dtype.itemsize for part in parts) * 5 // 4 + (2 << 20)


def load_blocks(scalars, slot_of, extras, dims, which, parts, whole, last):
    rows, cols, groups, per_row, slots, block = dims
    half = per_row // 2
    dtype = parts[0].dtype

    def body(*refs):
        sc, slots_own = refs[:2]
        part_refs = refs[2:2 + len(parts)]
        outs = refs[len(args):]
        out = outs[0]
        row = sc[0]
        for n in range(len(parts)):
            def move(i, carry, n=n):
                for s in range(slots):
                    out[n % 2 * half + i, row ^ which[n // 2], s] = part_refs[n][i, s].T
                return carry

            lax.fori_loop(0, half, move, 0, unroll=2)
        if last:
            diag = outs[1]
            col = sc[1]
            op = sc[2]
            row_i = lax.broadcasted_iota(jnp.int32, (block, block), 0)
            col_i = lax.broadcasted_iota(jnp.int32, (block, block), 1)
            ahead = jnp.where(op == 0, col_i - row_i, row_i - col_i) > 0
            for m in range(groups):
                for i in range(per_row):
                    value = out[i, col + cols * m, slots_own[m * per_row + i]].astype(jnp.float32)
                    diag[m, i] = jnp.where(ahead, value, 0.0).astype(dtype)

    vmem = pl.BlockSpec(memory_space=pltpu.VMEM)
    smem = pl.BlockSpec(memory_space=pltpu.SMEM)
    hbm = pl.BlockSpec(memory_space=pl.ANY)
    args = [scalars, slot_of, *parts, *extras] + ([] if whole is None else [whole])
    shapes = [jax.ShapeDtypeStruct((per_row, rows, slots, block, block), dtype)]
    if last:
        shapes.append(jax.ShapeDtypeStruct((groups, per_row, block, block), dtype))
    need = sum(math.prod(shape.shape) for shape in shapes) + sum(part.size for part in parts)
    return pl.pallas_call(
        body,
        out_shape=shapes,
        in_specs=[smem] * 2 + [vmem] * len(parts) + [hbm] * (len(args) - 2 - len(parts)),
        out_specs=[vmem] * len(shapes),
        input_output_aliases={} if whole is None else {len(args) - 1: 0},
        compiler_params=pltpu.CompilerParams(vmem_limit_bytes=need * dtype.itemsize + (2 << 20)),
        name="load_blocks",
    )(*args)


def load_operator(scalars, slot_of, extras, dims, parts):
    early = [k for k in range(dims[0]) if (k >> 1) & ((k >> 1) - 1) == 0]
    late = [k for k in range(dims[0]) if k not in early]
    stages = [which for which in (early, late) if which]
    loaded = [None]
    for n, which in enumerate(stages):
        chosen = [part for k in which for part in parts[2 * k:2 * k + 2]]
        loaded = load_blocks(
            scalars, slot_of, extras if n == 0 else [], dims, which, chosen, loaded[0], n + 1 == len(stages)
        )
    return loaded


def step_kernel(kind, step, dims, scalars, table, operator, level, pivot, state, received):
    rows, cols, groups, per_row, slots, block, kept = dims
    lanes = groups * kept
    locals_here = per_row * groups
    flat = (per_row * lanes, block)
    tile = (per_row, lanes, block)

    def body(*refs):
        refs = list(refs)
        sc = refs.pop(0)
        idx = refs.pop(0)
        whole = refs.pop(0)
        diag = refs.pop(0)
        level_ref = refs.pop(0)
        pivot_ref = refs.pop(0)
        res_ref = refs.pop(0)
        sol_ref = refs.pop(0) if len(state) > 1 else None
        got = [refs.pop(0) for _ in received]
        if kind == "last":
            share, share_sent = refs.pop(0), refs.pop(0)
        else:
            sends = [refs.pop(0) for _ in range(cols)]
            out_state = refs.pop(0)
        xs, acc = refs
        lv = level_ref[...]
        res = res_ref[...]
        if got:
            total = got[0][...]
            for ref in got[1:]:
                total = total + ref[...].astype(jnp.float32)
        if kind == "solved":
            rounded = res.astype(jnp.bfloat16).astype(jnp.float32)
            y = jnp.where(lv == step, total + pivot_ref[...] * rounded, 0.0)
            sol = y if sol_ref is None else sol_ref[...] + y
            out_state[...] = sol
            source = y
        elif kind in ("updated", "last"):
            back = total.astype(jnp.bfloat16).astype(jnp.float32)
            res = jnp.where(lv > step, res - back, res)
            source = jnp.where(lv == step + 1, res, 0.0)
            if kind == "updated":
                out_state[...] = res
            else:
                done = sol_ref[...] + pivot_ref[...] * source.astype(jnp.bfloat16).astype(jnp.float32)
        else:
            out_state[...] = res
            source = jnp.where(lv == 0, res, 0.0)
        source = source.reshape(tile)
        lane_group = lax.broadcasted_iota(jnp.int32, (1, lanes, block), 1) // kept
        for shift in range(groups):
            moved = source
            if shift:
                moved = jnp.concatenate([source[:, lanes - shift * kept:], source[:, :lanes - shift * kept]], axis=1)
            for m in range(groups):
                mine = (m + groups - shift) % groups
                put = jnp.where(lane_group == m, moved, 0.0)
                for i in range(per_row):
                    xs[m, i * groups + mine] = put[i]
        for m in range(groups):
            xs[m, locals_here] = jnp.zeros((lanes, block), jnp.float32)
        acc[...] = jnp.zeros(acc.shape, jnp.float32)
        col = sc[1]
        which = 3 + 4 * (step + (1 if kind in ("updated", "last") else 0)) + (2 if kind == "solved" else 0)

        def contract(x, w):
            return lax.dot_general(
                x.astype(jnp.bfloat16), w, (((1,), (0,)), ((), ())), preferred_element_type=jnp.float32
            )

        def group(i, carry):
            for cc in range(cols):
                left = []
                right = []
                for m in range(groups):
                    k = cc + cols * m
                    for s in range(slots):
                        left.append(xs[m, idx[(i * rows + k) * slots + s]])
                        right.append(whole[i, k, s])
                acc[cc, i] = contract(jnp.concatenate(left, axis=1), jnp.concatenate(right, axis=0))
            left = [xs[m, i * groups + m] for m in range(groups)]
            right = [diag[m, i] for m in range(groups)]
            acc[col, i] += contract(jnp.concatenate(left, axis=1), jnp.concatenate(right, axis=0))
            return carry

        lax.fori_loop(sc[which], sc[which + 1], group, 0)
        if kind == "last":
            acc[col] += done.reshape(tile)
            for cc in range(cols):
                rows_of = acc[cc].reshape(flat)
                share[cc] = rows_of
                share_sent[cc] = rows_of.astype(share_sent.dtype)
            return
        for d in range(cols):
            sends[d][...] = acc[col ^ d].reshape(flat).astype(sends[d].dtype)

    vmem = pl.BlockSpec(memory_space=pltpu.VMEM)
    smem = pl.BlockSpec(memory_space=pltpu.SMEM)
    budget = vmem_budget(operator)
    args = [scalars, table] + list(operator) + [level, pivot, *state, *received]
    if kind == "last":
        whole_shape = (cols, *flat)
        out_shape = [
            jax.ShapeDtypeStruct(whole_shape, jnp.float32),
            jax.ShapeDtypeStruct(whole_shape, jnp.bfloat16),
        ]
    else:
        out_shape = (
            [jax.ShapeDtypeStruct(flat, jnp.float32)]
            + [jax.ShapeDtypeStruct(flat, jnp.bfloat16)] * (cols - 1)
            + [jax.ShapeDtypeStruct(flat, jnp.float32)]
        )
    out_specs = [vmem] * len(out_shape)
    scratch = [
        pltpu.VMEM((groups, locals_here + 1, lanes, block), jnp.float32),
        pltpu.VMEM((cols, per_row, lanes, block), jnp.float32),
    ]
    return pl.pallas_call(
        body,
        out_shape=out_shape,
        in_specs=[smem, smem] + [vmem] * (len(args) - 2),
        out_specs=out_specs,
        scratch_shapes=scratch,
        compiler_params=pltpu.CompilerParams(vmem_limit_bytes=budget),
    )(*args)


def shards(
    factor, inverse_pivot, lower_rhs, upper_rhs, snode_of_block, level_of_snode, slot_columns
):
    rows = lax.axis_size("row")
    cols = lax.axis_size("col")
    r = lax.axis_index("row")
    c = lax.axis_index("col")
    per_row, slots, block = factor.shape[:3]
    total = snode_of_block.shape[0]
    snodes = level_of_snode.shape[0]
    rhs_count = lower_rhs.shape[0]
    steps = min(6, snodes // 2)
    groups = rows // cols
    kept = 2 * rhs_count // rows
    locals_here = per_row * groups
    op = r % 2
    dims = (rows, cols, groups, per_row, slots, block)

    small = jnp.concatenate(
        [inverse_pivot, jnp.pad(slot_columns.astype(jnp.float32), ((0, 0), (0, block - slots)))], axis=1
    )
    parts, small = gather_rows(factor, small)

    blocks = jnp.arange(total, dtype=jnp.int32)
    onehot = snode_of_block[:, None] == jnp.arange(snodes, dtype=jnp.int32)[None, :]
    levels = jnp.sum(jnp.where(onehot, level_of_snode[None, :], 0), axis=1)
    levels = jnp.where(op == 0, levels, steps - 1 - levels)

    def look_up(values, index):
        return jnp.sum(jnp.where(index[..., None] == blocks, values, 0), axis=-1)

    small = flip_order(small, r)
    slot_ids = small[:, :, block:block + slots].astype(jnp.int32).transpose(1, 0, 2)
    row_ids = blocks.reshape(per_row, rows)
    valid = slot_ids < total
    slot_snode = look_up(snode_of_block, slot_ids)
    slot_level = look_up(levels, slot_ids)
    row_snode = look_up(snode_of_block, row_ids)[..., None]
    row_level = look_up(levels, row_ids)[..., None]
    before = jnp.where(op == 0, row_ids[..., None] - slot_ids, slot_ids - row_ids[..., None]) > 0
    active = valid & jnp.where(slot_snode == row_snode, before, row_level > slot_level)
    table = jnp.where(active, slot_ids // cols, locals_here).reshape(-1)

    own_small = lax.dynamic_index_in_dim(small.reshape(groups, cols, *small.shape[1:]), c, 1, keepdims=False)
    own_ids = jnp.arange(per_row, dtype=jnp.int32)[None, :] * rows + c + cols * jnp.arange(groups)[:, None]
    own_slots = own_small[:, :, block:block + slots].astype(jnp.int32)
    slot_of = jnp.sum(
        jnp.where(own_slots == own_ids[..., None], jnp.arange(slots, dtype=jnp.int32), 0), axis=-1
    ).reshape(-1)

    def lay(values):
        shape = (per_row, groups, kept, block)
        return jnp.broadcast_to(values.transpose(1, 0, 2)[:, :, None], shape).reshape(-1, block)

    pivot = lay(jnp.where(op == 0, 1.0, own_small[:, :, :block]))
    level = lay(jnp.broadcast_to(look_up(levels, own_ids)[..., None], (groups, per_row, block)))

    step_ids = jnp.arange(steps, dtype=jnp.int32)
    at = jnp.sum((levels[None, :] == step_ids[:, None]).astype(jnp.int32), axis=1)
    upto = jnp.sum((levels[None, :] <= step_ids[:, None]).astype(jnp.int32), axis=1)
    solve_low = jnp.where(op == 0, upto - at, total - upto)
    solve_high = solve_low + at
    update_low = jnp.where(op == 0, upto, 0)
    update_high = jnp.where(op == 0, total, total - upto)
    bounds = jnp.stack(
        [
            solve_low // rows,
            (solve_high + rows - 1) // rows,
            update_low // rows,
            (update_high + rows - 1) // rows,
        ],
        axis=1,
    ).reshape(-1)
    scalars = jnp.concatenate([jnp.stack([r, c, op]), bounds]).astype(jnp.int32)

    chosen = jnp.where(op == 0, lower_rhs, upper_rhs)
    chosen = lax.dynamic_slice_in_dim(chosen, (r // 2) * kept, kept, 0)
    chosen = chosen.reshape(kept, per_row, groups, block).transpose(1, 2, 0, 3).reshape(-1, block)

    operator = load_operator(scalars, slot_of, [table, level, pivot, chosen], dims, parts)
    run = functools.partial(
        step_kernel,
        dims=dims + (kept,),
        scalars=scalars,
        table=table,
        operator=operator,
        level=level,
        pivot=pivot,
    )

    def exchange(sends):
        got = [sends[0]]
        for d in range(1, cols):
            got.append(xor_permute(sends[d], "col", d))
        return got

    res = chosen
    *sends, res = run("first", 0, state=(res,), received=[])
    for step in range(steps - 1):
        *sends, sol = run("solved", step, state=(res, sol) if step else (res,), received=exchange(sends))
        if step + 2 < steps:
            *sends, res = run("updated", step, state=(res,), received=exchange(sends))
    share, share_sent = run("last", steps - 2, state=(res, sol), received=exchange(sends))

    mine, *others = exchange([share] + [share_sent] * (cols - 1))
    whole = mine
    for other in others:
        whole = whole + other.astype(jnp.float32)
    whole = whole.reshape(cols, per_row, groups, kept, block).transpose(2, 0, 1, 3, 4)
    whole = whole.reshape(rows, per_row * kept, block)
    got = lax.all_to_all(whole, "row", 0, 0).reshape(rows // 2, 2, per_row, kept, block)
    got = got.transpose(1, 0, 3, 2, 4).reshape(2, rhs_count, per_row, block)
    return got[0], got[1]


def solution(mesh):
    in_specs = (
        P("row", "col", None, None),
        P("row", None),
        P(None, "col", None),
        P(None, "col", None),
        P(),
        P(),
        P("row", "col"),
    )
    out_specs = (P(None, "row", None), P(None, "row", None))
    return jax.shard_map(shards, mesh=mesh, in_specs=in_specs, out_specs=out_specs, check_vma=False)
```
